32 devices in a mesh: dp: 16 (over z, y, x), tensor: 2 (over core).
Axes of the slice: x: 2, y: 2, z: 4, core: 2. Of those that a mesh axis runs over, the one named last changes fastest.
Arguments:
- hidden_in: bfloat16 [16, 2048, 768], P('dp', 'tensor'), may hold values from -6 to 6
- encoder_in: bfloat16 [16, 2048, 768], P('dp', 'tensor'), may hold values from -6 to 6
- cotangent: bfloat16 [16, 2048, 768], P('dp', 'tensor'), may hold values from -6 to 6
- segments: int32 [16, 2048], P('dp'), may hold values from 0 to 15, never falling along the last dimension, each value on 1 to 1024 neighbouring positions
- document_block: int32 [16, 16], P('dp'), may hold values from 0 to 3
- block_lengths: int32 [16, 4], P('dp'), may hold values from 1 to 512, as said below
- exit_flags: int32 [16, 2048], P('dp'), may hold values from 0 to 1, as said below
- targets: int32 [16, 256], P('dp'), may hold values from 0 to 32127
- self_gain: bfloat16 [768], P('dp'), may hold values from 0.5 to 1.5
- self_query: bfloat16 [768, 768], P('dp', 'tensor'), may hold values from -0.109375 to 0.109375
- self_key: bfloat16 [768, 768], P('dp', 'tensor'), may hold values from -0.109375 to 0.109375
- self_value: bfloat16 [768, 768], P('dp', 'tensor'), may hold values from -0.21875 to 0.21875
- self_output: bfloat16 [768, 768], P('tensor', 'dp'), may hold values from -0.4375 to 0.4375
- cross_gain: bfloat16 [768], P('dp'), may hold values from 0.5 to 1.5
- cross_query: bfloat16 [768, 768], P('dp', 'tensor'), may hold values from -0.109375 to 0.109375
- cross_key: bfloat16 [768, 768], P('dp', 'tensor'), may hold values from -0.109375 to 0.109375
- cross_value: bfloat16 [768, 768], P('dp', 'tensor'), may hold values from -0.21875 to 0.21875
- cross_output: bfloat16 [768, 768], P('tensor', 'dp'), may hold values from -0.4375 to 0.4375
- feed_gain: bfloat16 [768], P('dp'), may hold values from 0.5 to 1.5
- feed_gate: bfloat16 [768, 2048], P('dp', 'tensor'), may hold values from -0.21875 to 0.21875
- feed_upper: bfloat16 [768, 2048], P('dp', 'tensor'), may hold values from -0.21875 to 0.21875
- feed_down: bfloat16 [2048, 768], P('tensor', 'dp'), may hold values from -0.1875 to 0.1875
- exit_gain: bfloat16 [768], P('dp'), may hold values from 0.5 to 1.5
- embedding: bfloat16 [32128, 768], P('tensor', 'dp'), may hold values from -16 to 16
Outputs:
- output: bfloat16 [16, 2048, 768], P('dp', 'tensor')
- losses: float32 [16, 256], P('dp')
- input_grad: float32 [16, 2048, 768], P('dp', 'tensor')
- encoder_grad: float32 [16, 2048, 768], P('dp', 'tensor')
- self_gain_grad: float32 [768], P('dp')
- self_query_grad: float32 [768, 768], P('dp', 'tensor')
- self_key_grad: float32 [768, 768], P('dp', 'tensor')
- self_value_grad: float32 [768, 768], P('dp', 'tensor')
- self_output_grad: float32 [768, 768], P('tensor', 'dp')
- cross_gain_grad: float32 [768], P('dp')
- cross_query_grad: float32 [768, 768], P('dp', 'tensor')
- cross_key_grad: float32 [768, 768], P('dp', 'tensor')
- cross_value_grad: float32 [768, 768], P('dp', 'tensor')
- cross_output_grad: float32 [768, 768], P('tensor', 'dp')
- feed_gain_grad: float32 [768], P('dp')
- feed_gate_grad: float32 [768, 2048], P('dp', 'tensor')
- feed_upper_grad: float32 [768, 2048], P('dp', 'tensor')
- feed_down_grad: float32 [2048, 768], P('tensor', 'dp')
- exit_gain_grad: float32 [768], P('dp')
- embedding_grad: float32 [32128, 768], P('tensor', 'dp')
The draws below stay inside these ranges and needn't reach their ends.
Inputs may be any that keep to these rules, and one draw needn't show every extreme that they name: `segments`: numbers never fall along a sequence; every document has 1 to 1024 tokens and one has exactly 1024. `block_lengths`: in every sequence at least one block has all 512 places valid; the valid places of a block come first. `exit_flags`: exactly 256 tokens of each sequence are flagged.
All inputs are finite; a program needn't handle non-finite values.
Results may differ from the reference program's by a relative error of at most 0.029.
Values may be sent and summed in bfloat16 or wider, within the bound.
No kernel may reach another device: no remote copies, remote signals or barrier semaphores. Data moves between devices by JAX's collectives and lax.ppermute only.
A program may use at most 320 MiB of HBM per device.

```python
import math
import jax
import jax.numpy as jnp
import numpy as np
from jax import lax

D = 768
HEADS = 12
HEAD_DIM = 64
FF = 2048
VOCAB = 32128
SEQ = 2048
DOCS = 16
ENC_BLK = 4
ENC_LEN = 512
SEQS = 16
EXITS = 256
DOC_MOST = 1024


def draw_block_lengths(key, part):
    key_lengths, key_choice = jax.random.split(key)
    lengths = jax.random.randint(key_lengths, (SEQS, ENC_BLK), 1, ENC_LEN + 1)
    chosen = jax.random.randint(key_choice, (SEQS, 1), 0, ENC_BLK)
    complete = jnp.arange(ENC_BLK)[None, :] == chosen
    return jnp.where(complete, ENC_LEN, lengths).astype(jnp.int32)


def draw_exit_flags(key, part):
    pattern = jnp.broadcast_to((jnp.arange(SEQ) < EXITS).astype(jnp.int32), (SEQS, SEQ))
    return jax.random.permutation(key, pattern, axis=1, independent=True).astype(jnp.int32)


def set_ends(values, rng, least, top_value):
    longest = values.shape.index(max(values.shape))
    spots = []
    for shift in (0, 1):
        where = [jax.random.randint(jax.random.fold_in(rng, axis), (), 0, length) for axis, length in enumerate(values.shape)]
        where[longest] = (where[longest] + shift) % values.shape[longest]
        spots.append(tuple(where))
    return values.at[spots[0]].set(least).at[spots[1]].set(top_value)


def block_scale(stream_key, shape, shards, low, top_value):
    level = 1.0
    for position, parts in shards:
        heights = jax.random.uniform(jax.random.fold_in(jax.random.fold_in(stream_key, 6), position), (parts,), jnp.float32, low / len(shards), top_value / len(shards))
        level = level * jnp.repeat(jnp.exp(heights), shape[position] // parts).reshape((-1,) + (1,) * (len(shape) - 1 - position))
    return level


def rank_table(count, lean):
    portions = [(1 << 20) // math.isqrt(grade ** lean) + 1 for grade in range(1, count + 1)]
    deviation = 1 + sum(portions) // (1 << 30)
    return np.cumsum(np.array([max(1, weight // deviation) for weight in portions]))


def skewed_ids(rng, shape, count, lean):
    listing = rank_table(count, lean)
    ticket = jax.random.randint(jax.random.fold_in(rng, 1), shape, 0, int(listing[count - 1]))
    standing = jnp.searchsorted(jnp.asarray(listing, jnp.int32), ticket, side="right")
    return jax.random.permutation(jax.random.fold_in(rng, 2), count)[standing].astype(jnp.int32)


def profile(amount, total, bound, lean):
    weights = [(1 << 20) // math.isqrt(standing ** lean) + 1 for standing in range(2, amount + 1)]
    spare, counts = total - bound - (amount - 1), [1] * (amount - 1)
    while spare > 0:
        free = [i for i in range(amount - 1) if counts[i] < bound]
        whole, left = sum([weights[i] for i in free]), spare
        for i in free:
            addition = min(bound - counts[i], max(1, left * weights[i] // whole), spare)
            counts[i] = counts[i] + addition
            spare = spare - addition
    return np.array([bound] + counts)


def ragged_sizes(own_key, number_of, total, bound, lean):
    if number_of == 2:
        one = jax.random.randint(own_key, (), max(1, total - bound), min(bound, total - 1) + 1)
        return jnp.stack([one, total - one])
    tallies = jnp.asarray(profile(number_of, total, bound, lean), jnp.int32)
    pairs = (number_of - 1) // 2
    giver, taker = tallies[1:1 + 2 * pairs:2], tallies[2:2 + 2 * pairs:2]
    room = jnp.minimum(giver - 1, bound - taker)
    moved = jax.random.randint(jax.random.fold_in(own_key, 1), (pairs,), 0, 1 << 20) % (room + 1)
    tallies = tallies.at[1:1 + 2 * pairs:2].set(giver - moved).at[2:2 + 2 * pairs:2].set(taker + moved)
    return tallies[jax.random.permutation(jax.random.fold_in(own_key, 2), number_of)]


def noise(rng, shape, deviation, reach, pieces=(), held_as=jnp.bfloat16):
    values = deviation * jax.random.normal(rng, shape, jnp.float32)
    if pieces:
        values = values * block_scale(rng, shape, pieces, -0.22, 0.18)
    return jnp.clip(values, -reach, reach).astype(held_as)


def setup_inputs(seed: int = 0) -> dict:
    seeds = jax.random.split(jax.random.key(seed), 25)
    hidden_in = noise(seeds[0], (SEQS, SEQ, D), 1.0, 6.0, ((0, 16), (1, 2)))
    encoder_in = noise(seeds[1], (SEQS, ENC_BLK * ENC_LEN, D), 1.0, 6.0, ((0, 16), (1, 2)))
    cotangent = noise(seeds[2], (SEQS, SEQ, D), 1.0, 6.0, ((0, 16), (1, 2)))
    segments = jax.vmap(lambda own: jnp.searchsorted(jnp.cumsum(ragged_sizes(own, DOCS, SEQ, DOC_MOST, 2)), jnp.arange(SEQ), side="right"))(jax.random.split(seeds[3], SEQS)).reshape((SEQS, SEQ)).astype(jnp.int32)
    document_block = set_ends(jax.random.randint(seeds[4], (SEQS, DOCS), 0, ENC_BLK), jax.random.fold_in(seeds[4], 1), 0, ENC_BLK - 1).astype(jnp.int32)
    block_lengths = draw_block_lengths(jax.random.fold_in(seeds[24], 71), 0)
    exit_flags = draw_exit_flags(jax.random.fold_in(seeds[24], 71), 0)
    targets = set_ends(skewed_ids(seeds[7], (SEQS, EXITS), VOCAB, 2), jax.random.fold_in(seeds[7], 3), 0, VOCAB - 1).astype(jnp.int32)
    self_gain = jnp.clip(1.0 + 0.1 * jax.random.normal(seeds[8], (D,), jnp.float32), 0.5, 1.5).astype(jnp.bfloat16)
    self_query = noise(seeds[9], (D, HEADS * HEAD_DIM), (4 * D) ** -0.5, 0.109375, ((0, 16), (1, 2)))
    self_key = noise(seeds[10], (D, HEADS * HEAD_DIM), (4 * D) ** -0.5, 0.109375, ((0, 16), (1, 2)))
    self_value = noise(seeds[11], (D, HEADS * HEAD_DIM), D ** -0.5, 0.21875, ((0, 16), (1, 2)))
    self_output = noise(seeds[12], (HEADS * HEAD_DIM, D), (D // 4) ** -0.5, 0.4375, ((0, 2), (1, 16)))
    cross_gain = jnp.clip(1.0 + 0.1 * jax.random.normal(seeds[13], (D,), jnp.float32), 0.5, 1.5).astype(jnp.bfloat16)
    cross_query = noise(seeds[14], (D, HEADS * HEAD_DIM), (4 * D) ** -0.5, 0.109375, ((0, 16), (1, 2)))
    cross_key = noise(seeds[15], (D, HEADS * HEAD_DIM), (4 * D) ** -0.5, 0.109375, ((0, 16), (1, 2)))
    cross_value = noise(seeds[16], (D, HEADS * HEAD_DIM), D ** -0.5, 0.21875, ((0, 16), (1, 2)))
    cross_output = noise(seeds[17], (HEADS * HEAD_DIM, D), (D // 4) ** -0.5, 0.4375, ((0, 2), (1, 16)))
    feed_gain = jnp.clip(1.0 + 0.1 * jax.random.normal(seeds[18], (D,), jnp.float32), 0.5, 1.5).astype(jnp.bfloat16)
    feed_gate = noise(seeds[19], (D, FF), D ** -0.5, 0.21875, ((0, 16), (1, 2)))
    feed_upper = noise(seeds[20], (D, FF), D ** -0.5, 0.21875, ((0, 16), (1, 2)))
    feed_down = noise(seeds[21], (FF, D), (FF // 2) ** -0.5, 0.1875, ((0, 2), (1, 16)))
    exit_gain = jnp.clip(1.0 + 0.1 * jax.random.normal(seeds[22], (D,), jnp.float32), 0.5, 1.5).astype(jnp.bfloat16)
    embedding = noise(seeds[23], (VOCAB, D), 3.0, 16.0, ((0, 2), (1, 16)))
    return {"hidden_in": hidden_in, "encoder_in": encoder_in, "cotangent": cotangent, "segments": segments, "document_block": document_block, "block_lengths": block_lengths, "exit_flags": exit_flags, "targets": targets, "self_gain": self_gain, "self_query": self_query, "self_key": self_key, "self_value": self_value, "self_output": self_output, "cross_gain": cross_gain, "cross_query": cross_query, "cross_key": cross_key, "cross_value": cross_value, "cross_output": cross_output, "feed_gain": feed_gain, "feed_gate": feed_gate, "feed_upper": feed_upper, "feed_down": feed_down, "exit_gain": exit_gain, "embedding": embedding}


EPSILON = 1e-06
MASK_FILL = -1e+30
HIGHEST = lax.Precision.HIGHEST

@jax.custom_vjp
def low(v):
    return lax.optimization_barrier(v.astype(jnp.bfloat16)).astype(jnp.float32)

@jax.custom_vjp
def low_back(v):
    return v

def low_keep(v):
    return (low(v), None)

def low_pass(kept, grad):
    return (grad,)

def back_keep(v):
    return (v, None)

def back_low(kept, grad):
    return (low(grad),)
low.defvjp(low_keep, low_pass)
low_back.defvjp(back_keep, back_low)

def norm_scale(values, gain):
    inverse = lax.rsqrt(lax.optimization_barrier(jnp.mean(values * values, axis=-1, keepdims=True)) + EPSILON)
    return values * inverse * gain

def product(left, right):
    return jnp.dot(left, right, precision=HIGHEST)

def attention(queries, keys, values, row_code, row_limit, key_code, key_order):
    row_count = queries.shape[0]
    span_rows = min(512, row_count)
    block_count = row_count // span_rows
    key_heads = keys.reshape(-1, HEADS, HEAD_DIM)
    value_heads = values.reshape(-1, HEADS, HEAD_DIM)

    @jax.checkpoint
    def block_step(inputs):
        query_block, code_block, limit_block = inputs
        scores = low_back(jnp.einsum('qhd,khd->hqk', query_block, key_heads, precision=HIGHEST))
        allowed = (code_block[:, None] == key_code[None, :]) & (key_order[None, :] <= limit_block[:, None])
        scores = jnp.where(allowed[None], scores, MASK_FILL)
        weights = low(jax.nn.softmax(scores, axis=-1))
        mixed = jnp.einsum('hqk,khd->qhd', weights, value_heads, precision=HIGHEST)
        return mixed.reshape(span_rows, HEADS * HEAD_DIM)
    mixed = lax.map(block_step, (queries.reshape(block_count, span_rows, HEADS, HEAD_DIM), row_code.reshape(block_count, span_rows), row_limit.reshape(block_count, span_rows)))
    return mixed.reshape(row_count, HEADS * HEAD_DIM)

def layer(hidden, encoder, weights, seg_row, doc_row, length_row, exit_rows, target_row):
    self_gain, self_query, self_key, self_value, self_output, cross_gain, cross_query, cross_key, cross_value, cross_output, feed_gain, feed_gate, feed_upper, feed_down, exit_gain, embedding = weights
    positions = jnp.arange(SEQ, dtype=jnp.int32)
    normed = low(norm_scale(hidden, self_gain))
    queries = low_back(low(product(normed, self_query)))
    keys = low_back(low(product(normed, self_key)))
    values = low_back(low(product(normed, self_value)))
    mixed = low_back(low(attention(queries, keys, values, seg_row, positions, seg_row, positions)))
    first = hidden + low_back(product(mixed, self_output))
    normed = low(norm_scale(first, cross_gain))
    queries = low_back(low(product(normed, cross_query)))
    keys = low_back(low(product(encoder, cross_key)))
    values = low_back(low(product(encoder, cross_value)))
    key_block = jnp.arange(ENC_BLK * ENC_LEN, dtype=jnp.int32) // ENC_LEN
    key_place = jnp.arange(ENC_BLK * ENC_LEN, dtype=jnp.int32) % ENC_LEN
    key_order = jnp.where(key_place < length_row[key_block], 0, 1).astype(jnp.int32)
    query_block = doc_row[seg_row]
    mixed = low_back(low(attention(queries, keys, values, query_block, jnp.zeros((SEQ,), jnp.int32), key_block, key_order)))
    second = first + low_back(product(mixed, cross_output))
    normed = low(norm_scale(second, feed_gain))
    gate = low_back(product(normed, feed_gate))
    upper = low_back(product(normed, feed_upper))
    hidden_units = low_back(low(jax.nn.gelu(gate, approximate=True) * upper))
    result = second + low_back(product(hidden_units, feed_down))
    normed = low(norm_scale(result, exit_gain))
    chosen = normed[exit_rows]
    logits = low_back(product(chosen, embedding.T)) * D ** (-0.5)
    losses = jax.nn.logsumexp(logits, axis=1) - jnp.take_along_axis(logits, target_row[:, None], axis=1)[:, 0]
    return (result, losses)

def reference(hidden_in, encoder_in, cotangent, segments, document_block, block_lengths, exit_flags, targets, self_gain, self_query, self_key, self_value, self_output, cross_gain, cross_query, cross_key, cross_value, cross_output, feed_gain, feed_gate, feed_upper, feed_down, exit_gain, embedding):
    weights = tuple((matrix.astype(jnp.float32) for matrix in (self_gain, self_query, self_key, self_value, self_output, cross_gain, cross_query, cross_key, cross_value, cross_output, feed_gain, feed_gate, feed_upper, feed_down, exit_gain, embedding)))

    def step(totals, inputs):
        hidden, encoder, tangent, seg_row, doc_row, length_row, flag_row, target_row = inputs
        exit_rows = jnp.nonzero(flag_row, size=EXITS)[0].astype(jnp.int32)

        def forward(hidden_value, encoder_value, layer_weights):
            return layer(hidden_value, encoder_value, layer_weights, seg_row, doc_row, length_row, exit_rows, target_row)
        (result, losses), backward = jax.vjp(forward, hidden.astype(jnp.float32), encoder.astype(jnp.float32), weights)
        hidden_grad, encoder_grad, weight_grads = backward((tangent.astype(jnp.float32), jnp.ones_like(losses)))
        totals = tuple((total + update for total, update in zip(totals, weight_grads)))
        return (totals, (result.astype(jnp.bfloat16), losses, hidden_grad, encoder_grad))
    initial = tuple((jnp.zeros_like(matrix) for matrix in weights))
    totals, (result, losses, hidden_grad, encoder_grad) = lax.scan(step, initial, (hidden_in, encoder_in, cotangent, segments, document_block, block_lengths, exit_flags, targets))
    return (result, losses, hidden_grad, encoder_grad, totals[0], totals[1], totals[2], totals[3], totals[4], totals[5], totals[6], totals[7], totals[8], totals[9], totals[10], totals[11], totals[12], totals[13], totals[14], totals[15])
```

```python
import functools

import jax
import jax.numpy as jnp
from jax import lax
from jax.experimental import pallas as pl
from jax.experimental.pallas import tpu as pltpu
from jax.sharding import PartitionSpec as P

HEAD_DIM = 64
PAIR = 128
ENC_LEN = 512
EPSILON = 1e-06
MASK_FILL = -1e30
Q_ROWS = 256
K_ROWS = 256
EXIT_BITS = 4
LANES = 128

BF16 = jnp.bfloat16
F32 = jnp.float32


def contract(left, right, left_dim, right_dim):
    return lax.dot_general(
        left, right, (((left_dim,), (right_dim,)), ((), ())), preferred_element_type=F32
    )


def attend_kernel(
    visits, counts, bases, q_ref, k_ref, v_ref, lo_ref, hi_ref, o_ref, total_ref, v_turned, mixed
):
    v_turned[...] = v_ref[...].T
    blocks = q_ref.shape[0] // Q_ROWS
    slots = k_ref.shape[0] // K_ROWS
    first_head = lax.broadcasted_iota(jnp.int32, (Q_ROWS, PAIR), 1) < HEAD_DIM
    key_index = lax.broadcasted_iota(jnp.int32, (K_ROWS, 2 * Q_ROWS), 0)

    def query_step(block, unused):
        rows = pl.ds(pl.multiple_of(block * Q_ROWS, Q_ROWS), Q_ROWS)
        query = q_ref[rows, :]
        zero = jnp.zeros_like(query)
        both = jnp.concatenate(
            [jnp.where(first_head, query, zero), jnp.where(first_head, zero, query)], axis=0
        )
        low = lo_ref[pl.ds(block, 1), :]
        high = hi_ref[pl.ds(block, 1), :]
        low = jnp.concatenate([low, low], axis=1)
        high = jnp.concatenate([high, high], axis=1)
        mixed[...] = jnp.zeros_like(mixed)

        def key_step(turn, carry):
            peak, total = carry
            slot = visits[block * slots + turn]
            keys = pl.ds(pl.multiple_of(slot * K_ROWS, K_ROWS), K_ROWS)
            base = bases[slot]
            scores = contract(k_ref[keys, :], both, 1, 1)
            seen = (key_index >= low - base) & (key_index <= high - base)
            scores = jnp.where(seen, scores, MASK_FILL)
            newest = jnp.maximum(peak, jnp.max(scores, axis=0, keepdims=True))
            weights = jnp.exp(scores - newest)
            fade = jnp.exp(peak - newest)
            total = total * fade + jnp.sum(weights, axis=0, keepdims=True)
            weights = weights.astype(BF16)
            for head in range(2):
                own = pl.ds(head * HEAD_DIM, HEAD_DIM)
                cols = slice(head * Q_ROWS, (head + 1) * Q_ROWS)
                mixed[own, :] = mixed[own, :] * fade[:, cols] + contract(
                    v_turned[own, keys], weights[:, cols], 1, 0
                )
            return newest, total

        start = (jnp.full((1, 2 * Q_ROWS), MASK_FILL, F32), jnp.zeros((1, 2 * Q_ROWS), F32))
        peak, total = lax.fori_loop(0, counts[block], key_step, start)
        share = 1.0 / total
        log_total = peak + jnp.log(total)
        for head in range(2):
            own = pl.ds(head * HEAD_DIM, HEAD_DIM)
            cols = slice(head * Q_ROWS, (head + 1) * Q_ROWS)
            mixed[own, :] = mixed[own, :] * share[:, cols]
        o_ref[rows, :] = mixed[...].T.astype(BF16)
        total_ref[0, pl.ds(block, 1), :] = log_total
        return unused

    lax.fori_loop(0, blocks, query_step, 0)


def attend_back_kernel(
    visits,
    counts,
    bases,
    q_ref,
    k_ref,
    v_ref,
    go_ref,
    o_ref,
    total_ref,
    lo_ref,
    hi_ref,
    *rest,
):
    outs, (k_turned, gq, gk, gv) = rest[:-4], rest[-4:]
    k_turned[...] = k_ref[...].T
    gk[...] = jnp.zeros_like(gk)
    gv[...] = jnp.zeros_like(gv)
    blocks = q_ref.shape[0] // Q_ROWS
    slots = k_ref.shape[0] // K_ROWS
    first_head = lax.broadcasted_iota(jnp.int32, (Q_ROWS, PAIR), 1) < HEAD_DIM
    key_index = lax.broadcasted_iota(jnp.int32, (K_ROWS, 2 * Q_ROWS), 0)
    if len(outs) == 1:
        gq_out, gk_out, gv_out = (outs[0].at[:, pl.ds(i * PAIR, PAIR)] for i in range(3))
    else:
        gq_out = outs[0]
        gk_out, gv_out = (outs[1].at[:, pl.ds(i * PAIR, PAIR)] for i in range(2))

    def doubled(value):
        zero = jnp.zeros_like(value)
        return jnp.concatenate(
            [jnp.where(first_head, value, zero), jnp.where(first_head, zero, value)], axis=0
        )

    def query_step(block, unused):
        rows = pl.ds(pl.multiple_of(block * Q_ROWS, Q_ROWS), Q_ROWS)
        queries = doubled(q_ref[rows, :])
        grad = go_ref[rows, :]
        grads = doubled(grad)
        turned = (grad.astype(F32) * o_ref[rows, :].astype(F32)).T
        inner = jnp.concatenate(
            [
                jnp.sum(turned[:HEAD_DIM], axis=0, keepdims=True),
                jnp.sum(turned[HEAD_DIM:], axis=0, keepdims=True),
            ],
            axis=1,
        )
        low = lo_ref[pl.ds(block, 1), :]
        high = hi_ref[pl.ds(block, 1), :]
        low = jnp.concatenate([low, low], axis=1)
        high = jnp.concatenate([high, high], axis=1)
        log_total = total_ref[0, pl.ds(block, 1), :]
        gq[...] = jnp.zeros_like(gq)

        def key_step(turn, carry):
            slot = visits[block * slots + turn]
            keys = pl.ds(pl.multiple_of(slot * K_ROWS, K_ROWS), K_ROWS)
            base = bases[slot]
            scores = contract(k_ref[keys, :], queries, 1, 1)
            seen = (key_index >= low - base) & (key_index <= high - base)
            weights = jnp.exp(jnp.where(seen, scores, MASK_FILL) - log_total)
            slopes = contract(v_ref[keys, :], grads, 1, 1)
            slopes = (weights * (slopes - inner)).astype(BF16)
            gv[keys, :] += contract(weights.astype(BF16), grads, 1, 0)
            gk[keys, :] += contract(slopes, queries, 1, 0)
            for head in range(2):
                own = pl.ds(head * HEAD_DIM, HEAD_DIM)
                cols = slice(head * Q_ROWS, (head + 1) * Q_ROWS)
                gq[own, :] += contract(k_turned[own, keys], slopes[:, cols], 1, 0)
            return carry

        lax.fori_loop(0, counts[block], key_step, 0)
        gq_out[rows, :] = gq[...].T.astype(BF16)
        return unused

    lax.fori_loop(0, blocks, query_step, 0)
    gk_out[...] = gk[...].astype(BF16)
    gv_out[...] = gv[...].astype(BF16)


def columns_of(rows, width, at):
    return pl.BlockSpec((rows, width), at)


SMALL = pl.BlockSpec(memory_space=pltpu.SMEM)


def kernel_params():
    return pltpu.CompilerParams(
        dimension_semantics=("arbitrary",), vmem_limit_bytes=48 * 1024 * 1024
    )


def pair_specs(rows, fused):
    if fused:
        return [pl.BlockSpec((rows, PAIR), lambda p, i=i: (0, 3 * p + i)) for i in range(3)]
    return [pl.BlockSpec((rows, PAIR), lambda p: (0, p))] + [
        pl.BlockSpec((rows, PAIR), lambda p, i=i: (0, 2 * p + i)) for i in range(2)
    ]


def attend(queries, keys_values, plan):
    fused = keys_values is None
    rows = queries.shape[0]
    pairs = queries.shape[1] // (3 * PAIR if fused else PAIR)
    blocks = rows // Q_ROWS
    source = queries if fused else keys_values
    visits, counts, bases, low, high = plan
    whole = pl.BlockSpec((blocks, Q_ROWS), lambda p: (0, 0))
    area = rows * 640 * pairs * 2
    return pl.pallas_call(
        attend_kernel,
        grid=(pairs,),
        in_specs=[SMALL] * 3 + pair_specs(rows, fused) + [whole, whole],
        out_specs=[
            pl.BlockSpec((rows, PAIR), lambda p: (0, p)),
            pl.BlockSpec((1, blocks, 2 * Q_ROWS), lambda p: (p, 0, 0)),
        ],
        out_shape=[
            jax.ShapeDtypeStruct((rows, pairs * PAIR), BF16),
            jax.ShapeDtypeStruct((pairs, blocks, 2 * Q_ROWS), F32),
        ],
        scratch_shapes=[pltpu.VMEM((PAIR, rows), BF16), pltpu.VMEM((PAIR, Q_ROWS), F32)],
        compiler_params=kernel_params(),
        cost_estimate=pl.CostEstimate(
            flops=area * 4 * 256, bytes_accessed=rows * pairs * PAIR * 8, transcendentals=area
        ),
        name="attend",
    )(visits, counts, bases, queries, source, source, low, high)


def attend_back(queries, keys_values, grad_mixed, mixed, log_totals, plan):
    fused = keys_values is None
    rows = queries.shape[0]
    pairs = queries.shape[1] // (3 * PAIR if fused else PAIR)
    blocks = rows // Q_ROWS
    source = queries if fused else keys_values
    visits, counts, bases, low, high = plan
    whole = pl.BlockSpec((blocks, Q_ROWS), lambda p: (0, 0))
    one = pl.BlockSpec((rows, PAIR), lambda p: (0, p))
    area = rows * 640 * pairs * 2
    widths = (3,) if fused else (1, 2)
    outs = pl.pallas_call(
        attend_back_kernel,
        grid=(pairs,),
        in_specs=[SMALL] * 3
        + pair_specs(rows, fused)
        + [one, one, pl.BlockSpec((1, blocks, 2 * Q_ROWS), lambda p: (p, 0, 0)), whole, whole],
        out_specs=[pl.BlockSpec((rows, w * PAIR), lambda p: (0, p)) for w in widths],
        out_shape=[jax.ShapeDtypeStruct((rows, w * pairs * PAIR), BF16) for w in widths],
        scratch_shapes=[
            pltpu.VMEM((PAIR, rows), BF16),
            pltpu.VMEM((PAIR, Q_ROWS), F32),
            pltpu.VMEM((rows, PAIR), F32),
            pltpu.VMEM((rows, PAIR), F32),
        ],
        compiler_params=kernel_params(),
        cost_estimate=pl.CostEstimate(
            flops=area * 10 * 256, bytes_accessed=rows * pairs * PAIR * 16, transcendentals=area
        ),
        name="attend_back",
    )(visits, counts, bases, queries, source, source, grad_mixed, mixed, log_totals, low, high)
    return outs


def visit_plan(low, high, bases):
    blocks = low.reshape(-1, Q_ROWS)
    ends = high.reshape(-1, Q_ROWS)
    touched = (blocks[:, None, :] <= bases[None, :, None] + (K_ROWS - 1)) & (
        ends[:, None, :] >= bases[None, :, None]
    )
    touched = jnp.any(touched, axis=2).astype(jnp.int32)
    slots = bases.shape[0]
    index = jnp.arange(slots, dtype=jnp.int32)
    before = (index[None, :] < index[:, None]).astype(jnp.int32)
    rank = jnp.sum(touched[:, None, :] * before[None], axis=2)
    counts = jnp.sum(touched, axis=1)
    chosen = (rank[:, :, None] == index[None, None, :]) & (touched[:, :, None] > 0)
    visits = jnp.sum(jnp.where(chosen, index[None, :, None], 0), axis=1)
    return visits.reshape(-1), counts, bases, blocks, ends


def swap(value):
    return lax.ppermute(value, "tensor", [(0, 1), (1, 0)])


def cross(value, bit):
    size = lax.axis_size("dp")
    return lax.ppermute(value, "dp", [(i, i ^ (1 << bit)) for i in range(size)])


def bit_count():
    return lax.axis_size("dp").bit_length() - 1


def my_bits():
    me = lax.axis_index("dp")
    return [(me >> k) & 1 for k in range(bit_count())]


def rotations(bits):
    far, near = bits[-1], list(bits[:-1])
    return [[far] + near[i:] + near[:i] for i in range(3)]


def spread(own):
    return jnp.concatenate([own, swap(own)], axis=0)


def collect(part):
    half = part.shape[0] // 2
    return part[:half] + swap(part[half:].astype(BF16)).astype(F32)


def hyper_gather(shard, order):
    count = bit_count()
    bits = my_bits()
    high_first = list(range(count))[::-1]
    tail = list(shard.shape)
    held = jnp.zeros([2] * count + tail, shard.dtype)
    held = lax.dynamic_update_slice(
        held, shard.reshape([1] * count + tail), [bits[b] for b in high_first] + [0] * len(tail)
    )
    done = set()
    for bit in order:
        start = [0 if b in done else bits[b] for b in high_first]
        sizes = [2 if b in done else 1 for b in high_first]
        piece = lax.dynamic_slice(held, start + [0] * len(tail), sizes + tail)
        start[high_first.index(bit)] = 1 - bits[bit]
        held = lax.dynamic_update_slice(held, cross(piece, bit), start + [0] * len(tail))
        done.add(bit)
    return held.reshape([-1] + tail[1:])


def hyper_scatter(value, order):
    count = bit_count()
    bits = my_bits()
    left = list(range(count))[::-1]
    held = value.reshape([2] * count + [value.shape[0] >> count, value.shape[1]])
    for bit in order:
        axis = left.index(bit)
        mine = lax.dynamic_index_in_dim(held, bits[bit], axis, keepdims=False)
        other = lax.dynamic_index_in_dim(held, 1 - bits[bit], axis, keepdims=False)
        held = mine + cross(other.astype(BF16), bit).astype(F32)
        left.remove(bit)
    return held


def groups():
    size = lax.axis_size("dp")
    near = [[4 * z + i for i in range(4)] for z in range(size // 4)]
    far = [[4 * z + i for z in range(size // 4)] for i in range(4)]
    return near, far


def wide_gather(shard):
    near, far = groups()
    value = lax.all_gather(shard, "dp", axis=0, tiled=True, axis_index_groups=near)
    return lax.all_gather(value, "dp", axis=0, tiled=True, axis_index_groups=far)


def wide_scatter(value):
    near, far = groups()
    value = lax.psum_scatter(
        value, "dp", scatter_dimension=0, tiled=True, axis_index_groups=far
    )
    return lax.psum_scatter(value, "dp", scatter_dimension=0, tiled=True, axis_index_groups=near)


def relative_gather(own, order):
    seen = []
    held = own
    for bit in order:
        axis = sum(b > bit for b in seen)
        held = jnp.stack([held, cross(held, bit)], axis=axis)
        seen.append(bit)
    return held.reshape((-1,) + own.shape)


def relative_scatter(value, order, tail):
    left = sorted(order, reverse=True)
    held = value.reshape([2] * len(left) + list(tail))
    for bit in order:
        axis = left.index(bit)
        mine = lax.index_in_dim(held, 0, axis, keepdims=False)
        other = lax.index_in_dim(held, 1, axis, keepdims=False)
        held = mine.astype(F32) + cross(other.astype(BF16), bit).astype(F32)
        left.remove(bit)
    return held


def turn_over(value, bits_used):
    bits = my_bits()
    held = value.reshape([2] * len(bits_used) + list(value.shape[1:]))
    left = sorted(bits_used, reverse=True)
    for bit in bits_used:
        axis = left.index(bit)
        mine = lax.dynamic_index_in_dim(held, bits[bit], axis, keepdims=False)
        other = lax.dynamic_index_in_dim(held, 1 - bits[bit], axis, keepdims=False)
        came = cross(other, bit)
        first = bits[bit] == 0
        held = jnp.stack(
            [jnp.where(first, mine, came), jnp.where(first, came, mine)], axis=axis
        )
    return held.reshape(value.shape)


def norm_scale(values, gain):
    inverse = lax.rsqrt(jnp.mean(values * values, axis=-1, keepdims=True) + EPSILON)
    return values * inverse * gain


def norm_back(values, gain, grad):
    inverse = lax.rsqrt(jnp.mean(values * values, axis=-1, keepdims=True) + EPSILON)
    unit = values * inverse
    scaled = grad * gain
    inner = jnp.mean(scaled * unit, axis=-1, keepdims=True)
    return inverse * (scaled - unit * inner), jnp.sum(grad * unit, axis=0)


def gate_mix(gate, upper):
    return jax.nn.gelu(gate, approximate=True) * upper


def braid(parts):
    pieces = [part.reshape(part.shape[0], -1, PAIR) for part in parts]
    return jnp.stack(pieces, axis=2).reshape(parts[0].shape[0], -1)


def unbraid(value, count):
    pieces = value.reshape(value.shape[0], -1, count, PAIR)
    return [pieces[:, :, i].reshape(value.shape[0], -1) for i in range(count)]


def on_device(
    hidden_in,
    encoder_in,
    cotangent,
    segments,
    document_block,
    block_lengths,
    exit_flags,
    targets,
    self_gain,
    self_query,
    self_key,
    self_value,
    self_output,
    cross_gain,
    cross_query,
    cross_key,
    cross_value,
    cross_output,
    feed_gain,
    feed_gate,
    feed_upper,
    feed_down,
    exit_gain,
    embedding,
):
    core = lax.axis_index("tensor")
    seq_rows = segments.shape[1]
    half = seq_rows // 2
    exits = targets.shape[1]
    half_exits = exits // 2
    width = hidden_in.shape[2]
    inner = self_query.shape[1]
    feed = feed_gate.shape[1]
    vocab_local = embedding.shape[0]
    count = bit_count()
    exit_bits = list(range(min(EXIT_BITS, count)))
    exit_group = 1 << len(exit_bits)
    chunk = -(-vocab_local // (exit_group * LANES)) * LANES
    logit_scale = float(width) ** (-0.5)

    gains = jnp.stack([self_gain, cross_gain, feed_gain, exit_gain], axis=1)
    gains = jnp.pad(gains, ((0, 0), (0, LANES - 4)))
    first_shard = jnp.concatenate([gains, braid([self_query, self_key, self_value])], axis=1)
    orders = rotations(list(range(count)))
    third = (inner * 3 + LANES) // LANES // 3 * LANES
    cuts = [0, third, 2 * third, first_shard.shape[1]]
    first_all = [
        hyper_gather(first_shard[:, cuts[i] : cuts[i + 1]], orders[i]) for i in range(3)
    ]
    first_all = jnp.concatenate(first_all, axis=1)
    second_all = wide_gather(
        jnp.concatenate(
            [self_output.T, cross_query, braid([cross_key, cross_value]), cross_output.T], axis=1
        )
    )
    third_all = wide_gather(jnp.concatenate([feed_gate, feed_upper, feed_down.T], axis=1))
    gain_self, gain_cross, gain_feed, gain_exit = (
        first_all[:, i].astype(F32) for i in range(4)
    )
    w_self = first_all[:, LANES:]
    w_self_out = second_all[:, :inner]
    w_cross_q = second_all[:, inner : 2 * inner]
    w_cross_kv = second_all[:, 2 * inner : 4 * inner]
    w_cross_out = second_all[:, 4 * inner :]
    w_gate = third_all[:, :feed]
    w_upper = third_all[:, feed : 2 * feed]
    w_down = third_all[:, 2 * feed :]

    vocab_turned = jnp.pad(embedding.T, ((0, 0), (0, exit_group * chunk - vocab_local)))
    vocab_turned = vocab_turned.reshape(-1, exit_group, chunk).transpose(1, 0, 2)
    vocab_turned = turn_over(vocab_turned, exit_bits)
    vocab_turned = vocab_turned.reshape(-1, chunk)
    if exit_group < lax.axis_size("dp"):
        far = [
            [exit_group * z + i for z in range(lax.axis_size("dp") // exit_group)]
            for i in range(exit_group)
        ]
        vocab_turned = lax.all_gather(
            vocab_turned, "dp", axis=0, tiled=True, axis_index_groups=far
        )

    offset = core * half
    seg = segments[0]
    docs = jnp.arange(document_block.shape[1], dtype=jnp.int32)
    seg_own = lax.dynamic_slice_in_dim(seg, offset, half)
    seg_other = lax.dynamic_slice_in_dim(seg, half - offset, half)
    seg_rel = jnp.concatenate([seg_own, seg_other])
    place = jnp.arange(seq_rows, dtype=jnp.int32)
    position = jnp.where(place + offset < seq_rows, place + offset, place + offset - seq_rows)
    is_doc = seg_rel[:, None] == docs[None, :]
    doc_start = jnp.sum((seg[:, None] < docs[None, :]).astype(jnp.int32), axis=0)
    doc_low = document_block[0] * ENC_LEN
    is_block = document_block[0][:, None] == jnp.arange(block_lengths.shape[1])[None, :]
    doc_high = doc_low + jnp.sum(jnp.where(is_block, block_lengths[0][None, :], 0), axis=1) - 1
    self_low = jnp.sum(jnp.where(is_doc, doc_start[None, :], 0), axis=1)
    cross_low = jnp.sum(jnp.where(is_doc, doc_low[None, :], 0), axis=1)
    cross_high = jnp.sum(jnp.where(is_doc, doc_high[None, :], 0), axis=1)
    slots = jnp.arange(seq_rows // K_ROWS, dtype=jnp.int32) * K_ROWS + offset
    bases = jnp.where(slots < seq_rows, slots, slots - seq_rows)
    self_plan = visit_plan(self_low, position, bases)
    cross_plan = visit_plan(cross_low, cross_high, bases)

    flags = exit_flags[0]
    slot = jnp.cumsum(flags) - 1
    slot_own = lax.dynamic_slice_in_dim(slot, offset, half)
    flag_own = lax.dynamic_slice_in_dim(flags, offset, half)
    slot_offset = core * half_exits
    slot_names = jnp.arange(exits, dtype=jnp.int32) + slot_offset
    slot_names = jnp.where(slot_names < exits, slot_names, slot_names - exits)
    pick = ((slot_own[None, :] == slot_names[:, None]) & (flag_own[None, :] == 1)).astype(BF16)
    target_own = lax.dynamic_slice_in_dim(targets[0], slot_offset, half_exits)
    target_all = relative_gather(target_own.reshape(1, half_exits), exit_bits[::-1])
    target_all = jnp.concatenate([target_all, swap(target_all)], axis=0).reshape(-1)

    encoder_all = spread(encoder_in[0])
    start = hidden_in[0].astype(F32)
    normed_self = spread(norm_scale(start, gain_self).astype(BF16))
    self_qkv = contract(normed_self, w_self, 1, 0).astype(BF16)
    self_mixed, self_totals = attend(self_qkv, None, self_plan)
    first = start + collect(contract(self_mixed, w_self_out, 1, 1))
    cross_kv = contract(encoder_all, w_cross_kv, 1, 0).astype(BF16)
    normed_cross = spread(norm_scale(first, gain_cross).astype(BF16))
    cross_q = contract(normed_cross, w_cross_q, 1, 0).astype(BF16)
    cross_mixed, cross_totals = attend(cross_q, cross_kv, cross_plan)
    second = first + collect(contract(cross_mixed, w_cross_out, 1, 1))
    normed_feed = spread(norm_scale(second, gain_feed).astype(BF16))
    gate = contract(normed_feed, w_gate, 1, 0)
    upper = contract(normed_feed, w_upper, 1, 0)
    units = gate_mix(gate, upper).astype(BF16)
    result = second + collect(contract(units, w_down, 1, 1))
    output = result.astype(BF16)

    normed_exit = norm_scale(result, gain_exit).astype(BF16)
    picked = contract(pick, normed_exit, 1, 0).astype(BF16)
    chosen = picked[:half_exits] + swap(picked[half_exits:])
    exit_orders = rotations(exit_bits)
    piece = width // 3
    chosen_all = jnp.concatenate(
        [
            relative_gather(chosen[:, i * piece : (i + 1) * piece], exit_orders[i])
            for i in range(3)
        ],
        axis=2,
    ).reshape(-1, width)
    chosen_all = jnp.concatenate([chosen_all, swap(chosen_all)], axis=0)
    logits = contract(chosen_all, vocab_turned, 1, 0) * logit_scale
    member = lax.axis_index("dp") % exit_group
    local_name = member * chunk + jnp.arange(chunk, dtype=jnp.int32)
    present = local_name < vocab_local
    vocab_name = jnp.where(present, core * vocab_local + local_name, -1)
    logits = jnp.where(present[None, :], logits, MASK_FILL)
    hit = target_all[:, None] == vocab_name[None, :]
    peak = jnp.max(logits, axis=1)
    log_total = peak + jnp.log(jnp.sum(jnp.exp(logits - peak[:, None]), axis=1))
    hit_logit = jnp.sum(jnp.where(hit, logits, 0.0), axis=1)
    stats = jnp.stack([log_total, hit_logit])

    def joined(mine, came):
        largest = jnp.maximum(mine[0], came[0])
        total = largest + jnp.log(jnp.exp(mine[0] - largest) + jnp.exp(came[0] - largest))
        return jnp.stack([total, mine[1] + came[1]])

    def flip(value, axis):
        shaped = value.reshape([2, 2] + [2] * len(exit_bits) + [half_exits])
        low_index = lax.index_in_dim(shaped, 0, axis)
        high_index = lax.index_in_dim(shaped, 1, axis)
        return jnp.concatenate([high_index, low_index], axis=axis).reshape(value.shape)

    stats = joined(stats, swap(flip(stats, 1)))
    for bit in exit_bits:
        stats = joined(stats, cross(flip(stats, 1 + len(exit_bits) - bit), bit))
    log_total = stats[0]
    loss = (stats[0] - stats[1]).reshape(2, exit_group, half_exits)[:, 0]
    loss = jnp.where(core == 0, loss.reshape(-1), loss[::-1].reshape(-1))

    grad_logits = (
        logit_scale * (jnp.exp(logits - log_total[:, None]) - hit.astype(F32))
    ).astype(BF16)
    grad_chosen = contract(grad_logits, vocab_turned, 1, 1)
    rows = grad_chosen.shape[0] // 2
    grad_chosen = grad_chosen[:rows] + swap(grad_chosen[rows:].astype(BF16)).astype(F32)
    grad_chosen = jnp.concatenate(
        [
            relative_scatter(
                grad_chosen[:, i * piece : (i + 1) * piece],
                exit_orders[i][1:][::-1] + exit_orders[i][:1],
                (half_exits, piece),
            )
            for i in range(3)
        ],
        axis=1,
    ).astype(BF16)
    grad_chosen = jnp.concatenate([grad_chosen, swap(grad_chosen)], axis=0)
    grad_vocab = contract(chosen_all, grad_logits, 0, 0).astype(BF16)
    if exit_group < lax.axis_size("dp"):
        grad_vocab = lax.psum_scatter(
            grad_vocab, "dp", scatter_dimension=0, tiled=True, axis_index_groups=far
        )
    grad_vocab = turn_over(grad_vocab.reshape(exit_group, -1, chunk), exit_bits)
    grad_vocab = grad_vocab.transpose(1, 0, 2).reshape(-1, exit_group * chunk)
    grad_vocab = grad_vocab[:, :vocab_local].astype(F32).T

    grad_normed = contract(pick, grad_chosen, 0, 0)
    grad_part, gain_exit_grad = norm_back(result, gain_exit, grad_normed)
    grad_result = grad_part + cotangent[0].astype(F32)

    rows_low = spread(grad_result.astype(BF16))
    grad_down = contract(rows_low, units, 0, 0)
    grad_units = contract(rows_low, w_down, 1, 0).astype(BF16)
    unused, mix_back = jax.vjp(gate_mix, gate, upper)
    grad_gate, grad_upper = mix_back(grad_units.astype(F32))
    grad_gate = grad_gate.astype(BF16)
    grad_upper = grad_upper.astype(BF16)
    gate_grad = contract(normed_feed, grad_gate, 0, 0)
    upper_grad = contract(normed_feed, grad_upper, 0, 0)
    third_grad = wide_scatter(
        jnp.concatenate([gate_grad, upper_grad, grad_down], axis=1).astype(BF16)
    ).astype(F32)
    grad_normed = collect(contract(grad_gate, w_gate, 1, 1) + contract(grad_upper, w_upper, 1, 1))
    grad_part, gain_feed_grad = norm_back(second, gain_feed, grad_normed)
    grad_second = grad_result + grad_part

    rows_low = spread(grad_second.astype(BF16))
    cross_out_grad = contract(rows_low, cross_mixed, 0, 0)
    grad_mixed = contract(rows_low, w_cross_out, 1, 0).astype(BF16)
    grad_q, grad_kv = attend_back(
        cross_q, cross_kv, grad_mixed, cross_mixed, cross_totals, cross_plan
    )
    grad_normed = collect(contract(grad_q, w_cross_q, 1, 1))
    grad_part, gain_cross_grad = norm_back(first, gain_cross, grad_normed)
    grad_first = grad_second + grad_part
    cross_q_grad = contract(normed_cross, grad_q, 0, 0)
    cross_kv_grad = contract(encoder_all, grad_kv, 0, 0)
    encoder_grad = collect(contract(grad_kv, w_cross_kv, 1, 1))

    rows_low = spread(grad_first.astype(BF16))
    self_out_grad = contract(rows_low, self_mixed, 0, 0)
    second_grad = wide_scatter(
        jnp.concatenate(
            [self_out_grad, cross_q_grad, cross_kv_grad, cross_out_grad], axis=1
        ).astype(BF16)
    ).astype(F32)
    grad_mixed = contract(rows_low, w_self_out, 1, 0).astype(BF16)
    (grad_qkv,) = attend_back(self_qkv, None, grad_mixed, self_mixed, self_totals, self_plan)
    self_grad = contract(normed_self, grad_qkv, 0, 0)
    grad_normed = collect(contract(grad_qkv, w_self, 1, 1))
    grad_part, gain_self_grad = norm_back(start, gain_self, grad_normed)
    input_grad = grad_first + grad_part

    gain_grads = jnp.stack([gain_self_grad, gain_cross_grad, gain_feed_grad, gain_exit_grad])
    gain_grads = (gain_grads + swap(gain_grads)).reshape(4, -1, self_gain.shape[0])
    for bit in range(count):
        gain_grads = gain_grads + cross(gain_grads, bit)
    gain_grads = lax.dynamic_index_in_dim(
        gain_grads, lax.axis_index("dp"), 1, keepdims=False
    )
    self_orders = [order[1:][::-1] + order[:1] for order in orders]
    self_grad = [
        hyper_scatter(self_grad[:, i * inner : (i + 1) * inner], self_orders[i]) for i in range(3)
    ]
    self_q_grad, self_k_grad, self_v_grad = unbraid(jnp.concatenate(self_grad, axis=1), 3)
    cross_k_grad, cross_v_grad = unbraid(second_grad[:, 2 * inner : 4 * inner], 2)
    return (
        output[None],
        loss[None],
        input_grad[None],
        encoder_grad[None],
        gain_grads[0],
        self_q_grad,
        self_k_grad,
        self_v_grad,
        second_grad[:, :inner].T,
        gain_grads[1],
        second_grad[:, inner : 2 * inner],
        cross_k_grad,
        cross_v_grad,
        second_grad[:, 4 * inner :].T,
        gain_grads[2],
        third_grad[:, :feed],
        third_grad[:, feed : 2 * feed],
        third_grad[:, 2 * feed :].T,
        gain_grads[3],
        grad_vocab,
    )


def solution(mesh):
    rows = P("dp", "tensor", None)
    each = P("dp", None)
    gain = P("dp")
    into = P("dp", "tensor")
    back = P("tensor", "dp")
    weights = (
        (gain, into, into, into, back)
        + (gain, into, into, into, back)
        + (gain, into, into, back)
        + (gain, back)
    )
    return jax.shard_map(
        on_device,
        mesh=mesh,
        in_specs=(rows, rows, rows) + (each,) * 5 + weights,
        out_specs=(rows, each, rows, rows) + weights,
        check_vma=False,
    )
```
